32 devices in a mesh: groups: 2 (over x), loop: 16 (over z, y, core).
Axes of the slice: x: 2, y: 2, z: 4, core: 2. Of those that a mesh axis runs over, the one named last changes fastest.
Arguments:
- queries: bfloat16 [16384, 2048], P(('groups', 'loop')), parts along dimension 0, may hold values from -16 to 16, as said below
- key_rows: bfloat16 [16384, 2048], P(('groups', 'loop')), parts along dimension 0, may hold values from -12 to 12, as said below
- values: bfloat16 [16384, 2048], P(('groups', 'loop')), parts along dimension 0, may hold values from -24 to 24
Outputs:
- attended: bfloat16 [16384, 2048], P(('groups', 'loop')), parts along dimension 0
- profile: float32 [4096], P('groups'), parts along dimension 0
The draws below stay inside these ranges and needn't reach their ends.
There are 2 independent parts, one for each index of `groups`. The reference program is written for one: setup_inputs(seed, part) draws one part's arguments, and reference() takes and returns one part's arrays. A program takes and returns all parts, laid end to end along the dimension named above; each array names one. Nothing has to cross between parts.
Inputs may be any that keep to these rules, and one draw needn't show every extreme that they name: Real-valued queries. `key_rows`: Real-valued keys of order one.
All inputs are finite; a program needn't handle non-finite values.
Results may differ from the reference program's by a relative error of at most 0.0049.
Values may be sent and summed in bfloat16 or wider, within the bound.
A program may use at most 128 MiB of HBM per device.

```python
import math
import jax
import jax.numpy as jnp
from jax import lax

HEADS = 16
HEAD_DIM = 128
SHARD = 256
WINDOW = 2048
SHARDS_DEV = 2
HD = 2048
GENOME = 8192


def draw_key_rows(key, part):
    field = jnp.clip(2.0 * jax.random.normal(jax.random.fold_in(key, 1), (GENOME, HD), jnp.float32), -12.0, 12.0)
    return field.astype(jnp.bfloat16)


def draw_queries(key, part):
    field = jnp.clip(jax.random.normal(jax.random.fold_in(key, 3), (GENOME, HD), jnp.float32), -6.0, 6.0)
    return field.astype(jnp.bfloat16)


def level_of(own_key, shape, cuts, smallest, high):
    loudness, own = 1.0, jax.random.fold_in(own_key, 6)
    for dim, parts in cuts:
        draws = jnp.exp(jax.random.uniform(jax.random.fold_in(own, dim), (parts,), jnp.float32, smallest / len(cuts), high / len(cuts)))
        loudness = loudness * jnp.repeat(draws, shape[dim] // parts).reshape([-1 if axis == dim else 1 for axis in range(len(shape))])
    return loudness


def bell_draw(stream_key, shape, width, limit, cuts=(), kind=jnp.bfloat16):
    array = width * jax.random.normal(stream_key, shape, jnp.float32)
    if cuts:
        array = array * level_of(stream_key, shape, cuts, -0.22, 0.18)
    return jnp.clip(array, -limit, limit).astype(kind)


def setup_inputs(seed: int = 0, part: int = 0) -> dict:
    key_list = jax.random.split(jax.random.key(seed), 4)
    part_keys = jax.random.split(jax.random.fold_in(key_list[3], part), 4)
    queries = draw_queries(jax.random.fold_in(jax.random.fold_in(key_list[3], part), 71), part)
    key_rows = draw_key_rows(jax.random.fold_in(jax.random.fold_in(key_list[3], part), 71), part)
    values = bell_draw(part_keys[2], (GENOME, HD), 4.0, 24.0, ((0, 16),))
    return dict(queries=queries, key_rows=key_rows, values=values)


def attend(query_block, key_ext, value_ext):
    row_count = query_block.shape[0]
    ext_count = key_ext.shape[0]
    scale = HEAD_DIM ** (-0.5)
    query_pos = lax.broadcasted_iota(jnp.int32, (row_count, ext_count), 0)
    key_pos = lax.broadcasted_iota(jnp.int32, (row_count, ext_count), 1)
    allowed = (key_pos > query_pos) & (key_pos <= query_pos + WINDOW)

    def one_head(head_index, output_buf):
        column = head_index * HEAD_DIM
        q_head = lax.dynamic_slice_in_dim(query_block, column, HEAD_DIM, 1)
        k_head = lax.dynamic_slice_in_dim(key_ext, column, HEAD_DIM, 1)
        v_head = lax.dynamic_slice_in_dim(value_ext, column, HEAD_DIM, 1)
        scores = lax.dot_general(q_head, k_head, (((1,), (1,)), ((), ())), preferred_element_type=jnp.float32) * scale
        scores = jnp.where(allowed, scores, jnp.float32(-1e+30))
        top = lax.optimization_barrier(jnp.max(scores, axis=1, keepdims=True))
        expo = jnp.exp(scores - top)
        weights = (expo / lax.optimization_barrier(jnp.sum(expo, axis=1, keepdims=True))).astype(jnp.bfloat16)
        head_out = jnp.dot(weights, v_head, preferred_element_type=jnp.float32).astype(jnp.bfloat16)
        return lax.dynamic_update_slice_in_dim(output_buf, head_out, column, 1)
    return lax.fori_loop(0, HEADS, one_head, jnp.zeros(query_block.shape, jnp.bfloat16))

def reference(queries, key_rows, values):
    block = SHARDS_DEV * SHARD
    starts = jnp.arange(GENOME // block, dtype=jnp.int32) * block

    def one_block(start):
        query_block = lax.dynamic_slice_in_dim(queries, start, block, 0)
        index = ((start - WINDOW + jnp.arange(WINDOW + block, dtype=jnp.int32)) % GENOME).astype(jnp.int32)
        key_ext = jnp.take(key_rows, index, axis=0)
        value_ext = jnp.take(values, index, axis=0)
        return attend(query_block, key_ext, value_ext)
    attended = lax.map(one_block, starts).reshape(GENOME, HD)
    profile = lax.optimization_barrier(jnp.sum(attended.astype(jnp.float32), axis=0)) / math.sqrt(GENOME)
    return (attended, profile)
```

```python
import functools
import math

import jax
import jax.numpy as jnp
from jax import lax
from jax.experimental import pallas as pl
from jax.experimental.pallas import tpu as pltpu
from jax.sharding import PartitionSpec as P

HEADS = 16
HEAD_DIM = 128
WINDOW = 2048
MESH = pl.DeviceIdType.MESH
PLANE = 4
TILE = 256
AHEAD = 2
COEF = HEAD_DIM ** (-0.5) * math.log2(math.e)


def attend_tile(q, keys, vals):
    nt = (((1,), (1,)), ((), ()))
    s = lax.dot_general(q, keys, nt, preferred_element_type=jnp.float32)
    row = lax.broadcasted_iota(jnp.int32, (TILE, TILE), 0)
    col = lax.broadcasted_iota(jnp.int32, (TILE, TILE), 1)
    upper = col > row
    edge = jnp.where(upper, s[:, :TILE], s[:, WINDOW:])
    mid = s[:, TILE:WINDOW]
    top = jnp.maximum(
        jnp.max(mid, axis=1, keepdims=True), jnp.max(edge, axis=1, keepdims=True)
    )
    p_mid = jnp.exp2((mid - top) * COEF)
    p_edge = jnp.exp2((edge - top) * COEF)
    total = jnp.sum(p_mid, axis=1, keepdims=True) + jnp.sum(p_edge, axis=1, keepdims=True)
    p_first = jnp.where(upper, p_edge, 0.0).astype(jnp.bfloat16)
    p_last = jnp.where(upper, 0.0, p_edge).astype(jnp.bfloat16)
    p = jnp.concatenate([p_first, p_mid.astype(jnp.bfloat16), p_last], axis=1)
    out = jnp.dot(p, vals, preferred_element_type=jnp.float32)
    return (out / total).astype(jnp.bfloat16)


def kernel(
    n, q_ref, k_ref, v_ref, o_ref, prof_ref,
    q_buf, kv, sums, planes,
    q_sem, own_sem, z_send, y_send, c_send, recv, sum_send, sum_recv,
):
    rows = q_ref.shape[0]
    me = lax.axis_index("loop")
    a, b = me // PLANE, me % PLANE
    y, c = b // 2, b % 2
    y_peer = me + 2 - 4 * y
    c_peer = me + 1 - 2 * c
    z_peer = lax.rem(me + PLANE, n)
    base = me - b
    plane_count = n // PLANE

    def block(h, slot):
        return kv.at[h, :, pl.ds(pl.multiple_of(slot * rows, rows), rows), :]

    def own_copies(h):
        cols = pl.ds(pl.multiple_of(h * HEAD_DIM, HEAD_DIM), HEAD_DIM)
        mine = pl.ds(PLANE * rows, rows)
        return (
            pltpu.make_async_copy(k_ref.at[:, cols], kv.at[h, 0, mine, :], own_sem.at[0, h]),
            pltpu.make_async_copy(v_ref.at[:, cols], kv.at[h, 1, mine, :], own_sem.at[1, h]),
        )

    def send(h, src, dst, send_sem, peer):
        return pltpu.make_async_remote_copy(
            src_ref=block(h, src),
            dst_ref=block(h, dst),
            send_sem=send_sem,
            recv_sem=recv.at[dst, h],
            device_id={"loop": peer},
            device_id_type=MESH,
        )

    def z_copy(h):
        return send(h, PLANE, 0, z_send.at[h], z_peer)

    def y_copy(h):
        return send(h, jnp.where(y == 0, PLANE, 0), 2, y_send.at[h], y_peer)

    def c_near(h):
        return send(h, jnp.where(c == 0, PLANE, 2), 3, c_send.at[0, h], c_peer)

    def c_far(h):
        return send(h, jnp.where(c == 0, 2, 0), 1, c_send.at[1, h], c_peer)

    q_copy = pltpu.make_async_copy(q_ref, q_buf, q_sem)

    def load(h, carry):
        for copy in own_copies(h):
            copy.start()
        return carry

    lax.fori_loop(0, HEADS, load, 0)
    q_copy.start()

    barrier = pltpu.get_barrier_semaphore()
    for k in range(1, PLANE):
        pl.semaphore_signal(
            barrier, inc=1, device_id={"loop": base + lax.rem(b + k, PLANE)}, device_id_type=MESH
        )
    for k in range(1, plane_count):
        pl.semaphore_signal(
            barrier, inc=1, device_id={"loop": lax.rem(me + PLANE * k, n)}, device_id_type=MESH
        )
    pl.semaphore_wait(barrier, PLANE - 1 + plane_count - 1)

    for h in range(AHEAD):
        for copy in own_copies(h):
            copy.wait()
        z_copy(h).start()
    q_copy.wait()

    def compute(h):
        cols = pl.ds(pl.multiple_of(h * HEAD_DIM, HEAD_DIM), HEAD_DIM)
        partial = jnp.zeros((1, HEAD_DIM), jnp.float32)
        for tile in range(rows // TILE):
            at = pl.ds(tile * TILE, TILE)
            span = pl.ds(tile * TILE, TILE + WINDOW)
            out = attend_tile(q_buf[at, cols], kv[h, 0, span, :], kv[h, 1, span, :])
            o_ref[at, cols] = out
            partial += jnp.sum(out.astype(jnp.float32), axis=0, keepdims=True)
        sums[b, pl.ds(h, 1), :] = partial

    def step(t, carry):
        @pl.when(t < HEADS)
        def _():
            z_copy(t).wait_recv()
            y_copy(t).start()
            z_copy(t).wait_send()

            @pl.when(t + AHEAD < HEADS)
            def _():
                for copy in own_copies(t + AHEAD):
                    copy.wait()
                z_copy(t + AHEAD).start()

        @pl.when((t >= 1) & (t <= HEADS))
        def _():
            y_copy(t - 1).wait_recv()
            c_near(t - 1).start()
            c_far(t - 1).start()

        @pl.when(t >= 2)
        def _():
            c_near(t - 2).wait_recv()
            c_far(t - 2).wait_recv()
            compute(t - 2)

        return carry

    lax.fori_loop(0, HEADS + 2, step, 0)

    def exchange(buf, slot, peer, stage, index):
        return pltpu.make_async_remote_copy(
            src_ref=buf.at[slot],
            dst_ref=buf.at[slot],
            send_sem=sum_send.at[stage, index],
            recv_sem=sum_recv.at[stage, index],
            device_id={"loop": peer},
            device_id_type=MESH,
        )

    copies = [
        exchange(sums, b, base + lax.rem(b + k, PLANE), 0, k) for k in range(1, PLANE)
    ]
    for copy in copies:
        copy.start()

    def drain(h, carry):
        y_copy(h).wait_send()
        c_near(h).wait_send()
        c_far(h).wait_send()
        return carry

    lax.fori_loop(0, HEADS, drain, 0)
    for k, copy in enumerate(copies, 1):
        copy.wait_send()
        exchange(sums, lax.rem(b + PLANE - k, PLANE), me, 0, k).wait_recv()
    plane = sums[0]
    for k in range(1, PLANE):
        plane += sums[k]
    planes[a] = plane
    copies = [
        exchange(planes, a, lax.rem(me + PLANE * k, n), 1, k) for k in range(1, plane_count)
    ]
    for copy in copies:
        copy.start()
    for k, copy in enumerate(copies, 1):
        copy.wait_send()
        exchange(planes, lax.rem(a + plane_count - k, plane_count), me, 1, k).wait_recv()
    total = planes[0]
    for k in range(1, plane_count):
        total += planes[k]
    prof_ref[...] = total / math.sqrt(rows * n)


def body(n, queries, key_rows, values):
    rows, width = queries.shape
    plane_count = n // PLANE
    if rows * PLANE != WINDOW or n % PLANE or plane_count < 2:
        raise ValueError("unsupported sizes")
    stages = max(PLANE, plane_count)
    any_spec = pl.BlockSpec(memory_space=pl.ANY)
    vmem_spec = pl.BlockSpec(memory_space=pltpu.VMEM)
    dma = pltpu.SemaphoreType.DMA
    attended, profile = pl.pallas_call(
        functools.partial(kernel, n),
        out_shape=(
            jax.ShapeDtypeStruct((rows, width), jnp.bfloat16),
            jax.ShapeDtypeStruct((HEADS, HEAD_DIM), jnp.float32),
        ),
        in_specs=[any_spec] * 3,
        out_specs=(vmem_spec, vmem_spec),
        scratch_shapes=[
            pltpu.VMEM((rows, width), jnp.bfloat16),
            pltpu.VMEM((HEADS, 2, (PLANE + 1) * rows, HEAD_DIM), jnp.bfloat16),
            pltpu.VMEM((PLANE, HEADS, HEAD_DIM), jnp.float32),
            pltpu.VMEM((plane_count, HEADS, HEAD_DIM), jnp.float32),
            dma,
            dma((2, HEADS)),
            dma((HEADS,)),
            dma((HEADS,)),
            dma((2, HEADS)),
            dma((PLANE, HEADS)),
            dma((2, stages)),
            dma((2, stages)),
        ],
        compiler_params=pltpu.CompilerParams(
            collective_id=0, has_side_effects=True, vmem_limit_bytes=56 * 1024 * 1024
        ),
        name="ring_attention",
    )(queries, key_rows, values)
    return attended, profile.reshape(width)


def solution(mesh):
    n = mesh.shape["loop"]
    return jax.shard_map(
        lambda q, k, v: body(n, q, k, v),
        mesh=mesh,
        in_specs=(
            P(("groups", "loop"), None),
            P(("groups", "loop"), None),
            P(("groups", "loop"), None),
        ),
        out_specs=(P(("groups", "loop"), None), P("groups")),
        check_vma=False,
    )
```

```python
import functools
import math

import jax
import jax.numpy as jnp
from jax import lax
from jax.experimental import pallas as pl
from jax.experimental.pallas import tpu as pltpu
from jax.sharding import PartitionSpec as P

HEADS = 16
HEAD_DIM = 128
WINDOW = 2048
MESH = pl.DeviceIdType.MESH
PLANE = 4
TILE = 256
SPLIT = 1
LAG_Y = 2
LAG_C = 1
LOADED = 4
AHEAD = 4
COEF = HEAD_DIM ** (-0.5) * math.log2(math.e)


def weigh_tile(q, keys):
    nt = (((1,), (1,)), ((), ()))
    s = lax.dot_general(q, keys, nt, preferred_element_type=jnp.float32)
    row = lax.broadcasted_iota(jnp.int32, (TILE, TILE), 0)
    col = lax.broadcasted_iota(jnp.int32, (TILE, TILE), 1)
    upper = col > row
    edge = jnp.where(upper, s[:, :TILE], s[:, WINDOW:])
    mid = s[:, TILE:WINDOW]
    top = jnp.maximum(
        jnp.max(mid, axis=1, keepdims=True), jnp.max(edge, axis=1, keepdims=True)
    )
    p_mid = jnp.exp2((mid - top) * COEF)
    p_edge = jnp.exp2((edge - top) * COEF)
    total = jnp.sum(p_mid, axis=1, keepdims=True) + jnp.sum(p_edge, axis=1, keepdims=True)
    p_first = jnp.where(upper, p_edge, 0.0).astype(jnp.bfloat16)
    p_last = jnp.where(upper, 0.0, p_edge).astype(jnp.bfloat16)
    p = jnp.concatenate([p_first, p_mid.astype(jnp.bfloat16), p_last], axis=1)
    return p, 1.0 / total


def kernel(
    n, q_ref, k_ref, v_ref, o_ref, prof_ref,
    q_buf, kv, p_buf, inv, sums, planes,
    q_sem, own_sem, z_send, y_send, c_send, recv, sum_send, sum_recv,
):
    rows = q_ref.shape[0]
    me = lax.axis_index("loop")
    a, b = me // PLANE, me % PLANE
    y, c = b // 2, b % 2
    y_peer = me + 2 - 4 * y
    c_peer = me + 1 - 2 * c
    z_peer = lax.rem(me + PLANE, n)
    base = me - b
    plane_count = n // PLANE

    part = rows // SPLIT
    pieces = 2 * HEADS * SPLIT

    def block(p, slot):
        at = pl.multiple_of(slot * rows + lax.rem(p, SPLIT) * part, part)
        return kv.at[p // SPLIT, pl.ds(at, part), :]

    def own_start(r):
        cols = pl.ds(pl.multiple_of((r // 2) * HEAD_DIM, HEAD_DIM), HEAD_DIM)
        mine = kv.at[r, pl.ds(PLANE * rows, rows), :]

        @pl.when(lax.rem(r, 2) == 0)
        def _():
            pltpu.make_async_copy(k_ref.at[:, cols], mine, own_sem.at[r]).start()

        @pl.when(lax.rem(r, 2) == 1)
        def _():
            pltpu.make_async_copy(v_ref.at[:, cols], mine, own_sem.at[r]).start()

    def own_wait(p):
        mine = pl.ds(PLANE * rows, rows)
        pltpu.make_async_copy(
            k_ref.at[:, pl.ds(0, HEAD_DIM)], kv.at[p // SPLIT, mine, :], own_sem.at[p // SPLIT]
        ).wait()

    def send(p, src, dst, send_sem, peer):
        return pltpu.make_async_remote_copy(
            src_ref=block(p, src),
            dst_ref=block(p, dst),
            send_sem=send_sem,
            recv_sem=recv.at[dst, p],
            device_id={"loop": peer},
            device_id_type=MESH,
        )

    def z_copy(h):
        return send(h, PLANE, 0, z_send.at[h], z_peer)

    def y_copy(h):
        return send(h, jnp.where(y == 0, PLANE, 0), 2, y_send.at[h], y_peer)

    def c_near(h):
        return send(h, jnp.where(c == 0, PLANE, 2), 3, c_send.at[0, h], c_peer)

    def c_far(h):
        return send(h, jnp.where(c == 0, 2, 0), 1, c_send.at[1, h], c_peer)

    q_copy = pltpu.make_async_copy(q_ref, q_buf, q_sem)

    def load(r, carry):
        own_start(r)
        return carry

    for r in range(LOADED):
        own_start(jnp.int32(r))

    barrier = pltpu.get_barrier_semaphore()
    for k in range(1, PLANE):
        pl.semaphore_signal(
            barrier, inc=1, device_id={"loop": base + lax.rem(b + k, PLANE)}, device_id_type=MESH
        )
    for k in range(1, plane_count):
        pl.semaphore_signal(
            barrier, inc=1, device_id={"loop": lax.rem(me + PLANE * k, n)}, device_id_type=MESH
        )
    pl.semaphore_wait(barrier, PLANE - 1 + plane_count - 1)

    for p in range(AHEAD):
        if p % SPLIT == 0:
            own_wait(p)
        z_copy(p).start()
    q_copy.start()
    lax.fori_loop(LOADED, 2 * HEADS, load, 0)
    q_copy.wait()

    def weigh(h, tile):
        cols = pl.ds(pl.multiple_of(h * HEAD_DIM, HEAD_DIM), HEAD_DIM)
        p, scale = weigh_tile(
            q_buf[pl.ds(tile * TILE, TILE), cols],
            kv[2 * h, pl.ds(tile * TILE, TILE + WINDOW), :],
        )
        p_buf[tile] = p
        inv[tile] = scale

    def gather(h):
        cols = pl.ds(pl.multiple_of(h * HEAD_DIM, HEAD_DIM), HEAD_DIM)
        partial = jnp.zeros((1, HEAD_DIM), jnp.float32)
        for tile in range(rows // TILE):
            vals = kv[2 * h + 1, pl.ds(tile * TILE, TILE + WINDOW), :]
            out = jnp.dot(p_buf[tile], vals, preferred_element_type=jnp.float32)
            out = (out * inv[tile]).astype(jnp.bfloat16)
            o_ref[pl.ds(tile * TILE, TILE), cols] = out
            partial += jnp.sum(out.astype(jnp.float32), axis=0, keepdims=True)
        sums[b, pl.ds(h, 1), :] = partial

    def step(t, carry):
        @pl.when(t < pieces)
        def _():
            z_copy(t).wait_recv()
            y_copy(t).start()
            z_copy(t).wait_send()

            @pl.when(t + AHEAD < pieces)
            def _():
                @pl.when(lax.rem(t + AHEAD, SPLIT) == 0)
                def _():
                    own_wait(t + AHEAD)

                z_copy(t + AHEAD).start()

        @pl.when((t >= LAG_Y) & (t < pieces + LAG_Y))
        def _():
            y_copy(t - LAG_Y).wait_recv()
            c_near(t - LAG_Y).start()
            c_far(t - LAG_Y).start()

        @pl.when(t >= LAG_Y + LAG_C)
        def _():
            u = t - LAG_Y - LAG_C
            c_near(u).wait_recv()
            c_far(u).wait_recv()
            phase = lax.rem(u, 2 * SPLIT)
            head = u // (2 * SPLIT)
            for tile in range(rows // TILE):

                @pl.when(phase == SPLIT - 1)
                def _():
                    weigh(head, tile)

            @pl.when(phase == 2 * SPLIT - 1)
            def _():
                gather(head)

        return carry

    lax.fori_loop(0, pieces + LAG_Y + LAG_C, step, 0)

    def exchange(buf, slot, peer, stage, index):
        return pltpu.make_async_remote_copy(
            src_ref=buf.at[slot],
            dst_ref=buf.at[slot],
            send_sem=sum_send.at[stage, index],
            recv_sem=sum_recv.at[stage, index],
            device_id={"loop": peer},
            device_id_type=MESH,
        )

    copies = [
        exchange(sums, b, base + lax.rem(b + k, PLANE), 0, k) for k in range(1, PLANE)
    ]
    for copy in copies:
        copy.start()

    def drain(h, carry):
        y_copy(h).wait_send()
        c_near(h).wait_send()
        c_far(h).wait_send()
        return carry

    lax.fori_loop(0, pieces, drain, 0)
    for k, copy in enumerate(copies, 1):
        copy.wait_send()
        exchange(sums, lax.rem(b + PLANE - k, PLANE), me, 0, k).wait_recv()
    plane = sums[0]
    for k in range(1, PLANE):
        plane += sums[k]
    planes[a] = plane
    copies = [
        exchange(planes, a, lax.rem(me + PLANE * k, n), 1, k) for k in range(1, plane_count)
    ]
    for copy in copies:
        copy.start()
    for k, copy in enumerate(copies, 1):
        copy.wait_send()
        exchange(planes, lax.rem(a + plane_count - k, plane_count), me, 1, k).wait_recv()
    total = planes[0]
    for k in range(1, plane_count):
        total += planes[k]
    prof_ref[...] = total / math.sqrt(rows * n)


def body(n, queries, key_rows, values):
    rows, width = queries.shape
    plane_count = n // PLANE
    if rows * PLANE != WINDOW or n % PLANE or plane_count < 2:
        raise ValueError("unsupported sizes")
    pieces = 2 * HEADS * SPLIT
    stages = max(PLANE, plane_count)
    hbm_spec = pl.BlockSpec(memory_space=pltpu.HBM)
    vmem_spec = pl.BlockSpec(memory_space=pltpu.VMEM)
    dma = pltpu.SemaphoreType.DMA
    attended, profile = pl.pallas_call(
        functools.partial(kernel, n),
        out_shape=(
            jax.ShapeDtypeStruct((rows, width), jnp.bfloat16),
            jax.ShapeDtypeStruct((HEADS, HEAD_DIM), jnp.float32),
        ),
        in_specs=[hbm_spec] * 3,
        out_specs=(vmem_spec, vmem_spec),
        scratch_shapes=[
            pltpu.VMEM((rows, width), jnp.bfloat16),
            pltpu.VMEM((2 * HEADS, (PLANE + 1) * rows, HEAD_DIM), jnp.bfloat16),
            pltpu.VMEM((rows // TILE, TILE, TILE + WINDOW), jnp.bfloat16),
            pltpu.VMEM((rows // TILE, TILE, 1), jnp.float32),
            pltpu.VMEM((PLANE, HEADS, HEAD_DIM), jnp.float32),
            pltpu.VMEM((plane_count, HEADS, HEAD_DIM), jnp.float32),
            dma,
            dma((2 * HEADS,)),
            dma((pieces,)),
            dma((pieces,)),
            dma((2, pieces)),
            dma((PLANE, pieces)),
            dma((2, stages)),
            dma((2, stages)),
        ],
        compiler_params=pltpu.CompilerParams(
            collective_id=0, has_side_effects=True, vmem_limit_bytes=51 * 1024 * 1024
        ),
        name="ring_attention",
    )(queries, key_rows, values)
    return attended, profile.reshape(width)


def solution(mesh):
    n = mesh.shape["loop"]
    return jax.shard_map(
        lambda q, k, v: body(n, q, k, v),
        mesh=mesh,
        in_specs=(
            P(("groups", "loop"), None),
            P(("groups", "loop"), None),
            P(("groups", "loop"), None),
        ),
        out_specs=(P(("groups", "loop"), None), P("groups")),
        check_vma=False,
    )
```

```python
import functools
import math

import jax
import jax.numpy as jnp
from jax import lax
from jax.experimental import pallas as pl
from jax.experimental.pallas import tpu as pltpu
from jax.sharding import PartitionSpec as P

HEADS = 16
HEAD_DIM = 128
WINDOW = 2048
MESH = pl.DeviceIdType.MESH
PLANE = 4
TILE = 256
SPLIT = 1
LAG_Y = 3
LAG_C = 1
LOADED = 6
AHEAD = 6
COEF = HEAD_DIM ** (-0.5) * math.log2(math.e)


def weigh_tile(q, keys):
    nt = (((1,), (1,)), ((), ()))
    s = lax.dot_general(q, keys, nt, preferred_element_type=jnp.float32)
    row = lax.broadcasted_iota(jnp.int32, (TILE, TILE), 0)
    col = lax.broadcasted_iota(jnp.int32, (TILE, TILE), 1)
    upper = col > row
    edge = jnp.where(upper, s[:, :TILE], s[:, WINDOW:])
    mid = s[:, TILE:WINDOW]
    top = jnp.maximum(
        jnp.max(mid, axis=1, keepdims=True), jnp.max(edge, axis=1, keepdims=True)
    )
    p_mid = jnp.exp2((mid - top) * COEF)
    p_edge = jnp.exp2((edge - top) * COEF)
    total = jnp.sum(p_mid, axis=1, keepdims=True) + jnp.sum(p_edge, axis=1, keepdims=True)
    p_first = jnp.where(upper, p_edge, 0.0).astype(jnp.bfloat16)
    p_last = jnp.where(upper, 0.0, p_edge).astype(jnp.bfloat16)
    p = jnp.concatenate([p_first, p_mid.astype(jnp.bfloat16), p_last], axis=1)
    return p, 1.0 / total


def kernel(
    n, q_ref, k_ref, v_ref, o_ref, prof_ref,
    q_buf, kv, p_buf, inv, sums, planes, lasts,
    q_sem, own_sem, z_send, y_send, c_send, recv, sum_send, sum_recv,
):
    rows = q_ref.shape[0]
    me = lax.axis_index("loop")
    a, b = me // PLANE, me % PLANE
    y, c = b // 2, b % 2
    y_peer = me + 2 - 4 * y
    c_peer = me + 1 - 2 * c
    z_peer = lax.rem(me + PLANE, n)
    base = me - b
    plane_count = n // PLANE

    part = rows // SPLIT
    pieces = 2 * HEADS * SPLIT

    def block(p, slot):
        at = pl.multiple_of(slot * rows + lax.rem(p, SPLIT) * part, part)
        return kv.at[p // SPLIT, pl.ds(at, part), :]

    def own_start(r):
        cols = pl.ds(pl.multiple_of((r // 2) * HEAD_DIM, HEAD_DIM), HEAD_DIM)
        mine = kv.at[r, pl.ds(PLANE * rows, rows), :]

        @pl.when(lax.rem(r, 2) == 0)
        def _():
            pltpu.make_async_copy(k_ref.at[:, cols], mine, own_sem.at[r]).start()

        @pl.when(lax.rem(r, 2) == 1)
        def _():
            pltpu.make_async_copy(v_ref.at[:, cols], mine, own_sem.at[r]).start()

    def own_wait(p):
        mine = pl.ds(PLANE * rows, rows)
        pltpu.make_async_copy(
            k_ref.at[:, pl.ds(0, HEAD_DIM)], kv.at[p // SPLIT, mine, :], own_sem.at[p // SPLIT]
        ).wait()

    def send(p, src, dst, send_sem, peer):
        return pltpu.make_async_remote_copy(
            src_ref=block(p, src),
            dst_ref=block(p, dst),
            send_sem=send_sem,
            recv_sem=recv.at[dst, p],
            device_id={"loop": peer},
            device_id_type=MESH,
        )

    def z_copy(h):
        return send(h, PLANE, 0, z_send.at[h], z_peer)

    def y_copy(h):
        return send(h, jnp.where(y == 0, PLANE, 0), 2, y_send.at[h], y_peer)

    def c_near(h):
        return send(h, jnp.where(c == 0, PLANE, 2), 3, c_send.at[0, h], c_peer)

    def c_far(h):
        return send(h, jnp.where(c == 0, 2, 0), 1, c_send.at[1, h], c_peer)

    q_copy = pltpu.make_async_copy(q_ref, q_buf, q_sem)

    def load(r, carry):
        own_start(r)
        return carry

    for r in range(LOADED):
        own_start(jnp.int32(r))

    barrier = pltpu.get_barrier_semaphore()
    for k in range(1, n):
        pl.semaphore_signal(
            barrier, inc=1, device_id={"loop": lax.rem(me + k, n)}, device_id_type=MESH
        )
    pl.semaphore_wait(barrier, n - 1)

    for p in range(AHEAD):
        if p % SPLIT == 0:
            own_wait(p)
        z_copy(p).start()
    q_copy.start()
    lax.fori_loop(LOADED, 2 * HEADS, load, 0)
    q_copy.wait()

    def weigh(h, tile):
        cols = pl.ds(pl.multiple_of(h * HEAD_DIM, HEAD_DIM), HEAD_DIM)
        p, scale = weigh_tile(
            q_buf[pl.ds(tile * TILE, TILE), cols],
            kv[2 * h, pl.ds(tile * TILE, TILE + WINDOW), :],
        )
        p_buf[tile] = p
        inv[tile] = scale

    def gather(h):
        cols = pl.ds(pl.multiple_of(h * HEAD_DIM, HEAD_DIM), HEAD_DIM)
        partial = jnp.zeros((1, HEAD_DIM), jnp.float32)
        for tile in range(rows // TILE):
            vals = kv[2 * h + 1, pl.ds(tile * TILE, TILE + WINDOW), :]
            out = jnp.dot(p_buf[tile], vals, preferred_element_type=jnp.float32)
            out = (out * inv[tile]).astype(jnp.bfloat16)
            o_ref[pl.ds(tile * TILE, TILE), cols] = out
            partial += jnp.sum(out.astype(jnp.float32), axis=0, keepdims=True)

        @pl.when(h < HEADS - 1)
        def _():
            sums[b, pl.ds(h, 1), :] = partial

        @pl.when(h == HEADS - 2)
        def _():
            for k in range(1, PLANE):
                plane_copy(k).start()

        @pl.when(h == HEADS - 1)
        def _():
            lasts[me] = partial
            for k in range(1, n):
                last_copy(k).start()

    def exchange(buf, slot, peer, stage, index):
        return pltpu.make_async_remote_copy(
            src_ref=buf.at[slot],
            dst_ref=buf.at[slot],
            send_sem=sum_send.at[stage, index],
            recv_sem=sum_recv.at[stage, index],
            device_id={"loop": peer},
            device_id_type=MESH,
        )

    def plane_copy(k):
        return exchange(sums, b, base + lax.rem(b + k, PLANE), 0, k)

    def chain_copy(k):
        return exchange(planes, a, lax.rem(me + PLANE * k, n), 1, k)

    def last_copy(k):
        return exchange(lasts, me, lax.rem(me + k, n), 2, k)

    def add_plane():
        for k in range(1, PLANE):
            plane_copy(k).wait_send()
            exchange(sums, lax.rem(b + PLANE - k, PLANE), me, 0, k).wait_recv()
        plane = sums[0]
        for k in range(1, PLANE):
            plane += sums[k]
        planes[a] = plane
        for k in range(1, plane_count):
            chain_copy(k).start()

    def step(t, carry):
        @pl.when(t < pieces)
        def _():
            z_copy(t).wait_recv()
            y_copy(t).start()
            z_copy(t).wait_send()

            @pl.when(t + AHEAD < pieces)
            def _():
                @pl.when(lax.rem(t + AHEAD, SPLIT) == 0)
                def _():
                    own_wait(t + AHEAD)

                z_copy(t + AHEAD).start()

        @pl.when((t >= LAG_Y) & (t < pieces + LAG_Y))
        def _():
            y_copy(t - LAG_Y).wait_recv()
            c_near(t - LAG_Y).start()
            c_far(t - LAG_Y).start()

        @pl.when(t >= LAG_Y + LAG_C)
        def _():
            u = t - LAG_Y - LAG_C
            c_near(u).wait_recv()
            c_far(u).wait_recv()
            phase = lax.rem(u, 2 * SPLIT)
            head = u // (2 * SPLIT)
            for tile in range(rows // TILE):

                @pl.when(phase == SPLIT - 1)
                def _():
                    weigh(head, tile)

            @pl.when((phase == SPLIT - 1) & (head == HEADS - 1))
            def _():
                add_plane()

            @pl.when(phase == 2 * SPLIT - 1)
            def _():
                gather(head)

        return carry

    sums[b, pl.ds(HEADS - 1, 1), :] = jnp.zeros((1, HEAD_DIM), jnp.float32)
    lax.fori_loop(0, pieces + LAG_Y + LAG_C, step, 0)

    def drain(h, carry):
        y_copy(h).wait_send()
        c_near(h).wait_send()
        c_far(h).wait_send()
        return carry

    lax.fori_loop(0, pieces, drain, 0)
    for k in range(1, plane_count):
        chain_copy(k).wait_send()
        exchange(planes, lax.rem(a + plane_count - k, plane_count), me, 1, k).wait_recv()
    total = planes[0]
    for k in range(1, plane_count):
        total += planes[k]
    prof_ref[...] = total / math.sqrt(rows * n)
    for k in range(1, n):
        last_copy(k).wait_send()
        exchange(lasts, lax.rem(me + n - k, n), me, 2, k).wait_recv()
    last = lasts[0]
    for k in range(1, n):
        last += lasts[k]
    prof_ref[pl.ds(HEADS - 1, 1), :] = last / math.sqrt(rows * n)


def body(n, queries, key_rows, values):
    rows, width = queries.shape
    plane_count = n // PLANE
    if rows * PLANE != WINDOW or n % PLANE or plane_count < 2:
        raise ValueError("unsupported sizes")
    pieces = 2 * HEADS * SPLIT
    hbm_spec = pl.BlockSpec(memory_space=pltpu.HBM)
    vmem_spec = pl.BlockSpec(memory_space=pltpu.VMEM)
    dma = pltpu.SemaphoreType.DMA
    attended, profile = pl.pallas_call(
        functools.partial(kernel, n),
        out_shape=(
            jax.ShapeDtypeStruct((rows, width), jnp.bfloat16),
            jax.ShapeDtypeStruct((HEADS, HEAD_DIM), jnp.float32),
        ),
        in_specs=[hbm_spec] * 3,
        out_specs=(vmem_spec, vmem_spec),
        scratch_shapes=[
            pltpu.VMEM((rows, width), jnp.bfloat16),
            pltpu.VMEM((2 * HEADS, (PLANE + 1) * rows, HEAD_DIM), jnp.bfloat16),
            pltpu.VMEM((rows // TILE, TILE, TILE + WINDOW), jnp.bfloat16),
            pltpu.VMEM((rows // TILE, TILE, 1), jnp.float32),
            pltpu.VMEM((PLANE, HEADS, HEAD_DIM), jnp.float32),
            pltpu.VMEM((plane_count, HEADS, HEAD_DIM), jnp.float32),
            pltpu.VMEM((n, 1, HEAD_DIM), jnp.float32),
            dma,
            dma((2 * HEADS,)),
            dma((pieces,)),
            dma((pieces,)),
            dma((2, pieces)),
            dma((PLANE, pieces)),
            dma((3, n)),
            dma((3, n)),
        ],
        compiler_params=pltpu.CompilerParams(
            collective_id=0, has_side_effects=True, vmem_limit_bytes=51 * 1024 * 1024
        ),
        name="ring_attention",
    )(queries, key_rows, values)
    return attended, profile.reshape(width)


def solution(mesh):
    n = mesh.shape["loop"]
    return jax.shard_map(
        lambda q, k, v: body(n, q, k, v),
        mesh=mesh,
        in_specs=(
            P(("groups", "loop"), None),
            P(("groups", "loop"), None),
            P(("groups", "loop"), None),
        ),
        out_specs=(P(("groups", "loop"), None), P("groups")),
        check_vma=False,
    )
```
